32 devices in a mesh: dp: 4 (over y, x), fsdp: 8 (over z, core).
Axes of the slice: x: 2, y: 2, z: 4, core: 2. Of those that a mesh axis runs over, the one named last changes fastest.
Arguments:
- tokens: bfloat16 [32768, 768], P(('dp', 'fsdp')), may hold values from -6 to 6
- lengths: int32 [64], P(('dp', 'fsdp')), may hold values from 1 to 512, 20480 in all
- cotangent: bfloat16 [32768, 768], P(('dp', 'fsdp')), may hold values from -6 to 6
- weight_qkv: float32 [576, 768], P(None, ('dp', 'fsdp')), may hold values from -0.4375 to 0.4375
- weight_out: float32 [768, 768], P(None, ('dp', 'fsdp')), may hold values from -1.25 to 1.25
- weight_in: float32 [768, 768], P(None, ('dp', 'fsdp')), may hold values from -0.4375 to 0.4375
- weight_down: float32 [768, 768], P(None, ('dp', 'fsdp')), may hold values from -0.21875 to 0.21875
- biases: float32 [10, 768], P(None, ('dp', 'fsdp')), may hold values from -1.2 to 1.2
- gains: float32 [2, 768], P(None, ('dp', 'fsdp')), may hold values from 0.5 to 1.5
- first_qkv: float32 [576, 768], P(None, ('dp', 'fsdp')), may hold values from -448 to 448
- first_out: float32 [768, 768], P(None, ('dp', 'fsdp')), may hold values from -80 to 80
- first_in: float32 [768, 768], P(None, ('dp', 'fsdp')), may hold values from -192 to 192
- first_down: float32 [768, 768], P(None, ('dp', 'fsdp')), may hold values from -448 to 448
- first_biases: float32 [10, 768], P(None, ('dp', 'fsdp')), may hold values from -384 to 384
- first_gains: float32 [2, 768], P(None, ('dp', 'fsdp')), may hold values from -512 to 512
- second_qkv: float32 [576, 768], P(None, ('dp', 'fsdp')), may hold values from 5461 to 21845
- second_out: float32 [768, 768], P(None, ('dp', 'fsdp')), may hold values from 163 to 655
- second_in: float32 [768, 768], P(None, ('dp', 'fsdp')), may hold values from 1092 to 4369
- second_down: float32 [768, 768], P(None, ('dp', 'fsdp')), may hold values from 5461 to 21845
- second_biases: float32 [10, 768], P(None, ('dp', 'fsdp')), may hold values from 3640 to 14563
- second_gains: float32 [2, 768], P(None, ('dp', 'fsdp')), may hold values from 8192 to 32768
Outputs:
- output: bfloat16 [32768, 768], P(('dp', 'fsdp'))
- tokens_grad: bfloat16 [32768, 768], P(('dp', 'fsdp'))
- new_first_qkv: float32 [576, 768], P(None, ('dp', 'fsdp'))
- new_first_out: float32 [768, 768], P(None, ('dp', 'fsdp'))
- new_first_in: float32 [768, 768], P(None, ('dp', 'fsdp'))
- new_first_down: float32 [768, 768], P(None, ('dp', 'fsdp'))
- new_first_biases: float32 [10, 768], P(None, ('dp', 'fsdp'))
- new_first_gains: float32 [2, 768], P(None, ('dp', 'fsdp'))
- new_second_qkv: float32 [576, 768], P(None, ('dp', 'fsdp'))
- new_second_out: float32 [768, 768], P(None, ('dp', 'fsdp'))
- new_second_in: float32 [768, 768], P(None, ('dp', 'fsdp'))
- new_second_down: float32 [768, 768], P(None, ('dp', 'fsdp'))
- new_second_biases: float32 [10, 768], P(None, ('dp', 'fsdp'))
- new_second_gains: float32 [2, 768], P(None, ('dp', 'fsdp'))
- new_weight_qkv: float32 [576, 768], P(None, ('dp', 'fsdp'))
- new_weight_out: float32 [768, 768], P(None, ('dp', 'fsdp'))
- new_weight_in: float32 [768, 768], P(None, ('dp', 'fsdp'))
- new_weight_down: float32 [768, 768], P(None, ('dp', 'fsdp'))
- new_weight_biases: float32 [10, 768], P(None, ('dp', 'fsdp'))
- new_weight_gains: float32 [2, 768], P(None, ('dp', 'fsdp'))
The draws below stay inside these ranges and needn't reach their ends.
Inputs may be any that keep to these rules, and one draw needn't show every extreme that they name: The tokens of a sequence at positions below its length are real, the rest padding; the lengths sum to 20480 and at least one sequence is full.
All inputs are finite; a program needn't handle non-finite values. No bound on the sum of `lengths` on one device may be relied on, other than what follows from the above.
Results may differ from the reference program's by a relative error of at most 0.013.
The reference program's roundings to bfloat16 on the way count: a program that leaves them out, or rounds other values in their place, can miss the bound.
Values may be sent and summed in bfloat16 or wider, within the bound.
A program may use at most 256 MiB of HBM per device.

```python
import math
import jax
import jax.numpy as jnp
import numpy as np
from jax import lax

D = 768
HEADS = 12
HEAD = 64
FF = 3072
GROUPS = 4
SEQ = 512
STEP = 5
SEQ_DEV = 2
SEQS = 64
TOKENS = 32768


def block_levels(stream_key, extent, pieces, smallest, largest):
    loudness, own = 1.0, jax.random.fold_in(stream_key, 6)
    for axis_at, blocks in pieces:
        draws = jnp.exp(jax.random.uniform(jax.random.fold_in(own, axis_at), (blocks,), jnp.float32, smallest / len(pieces), largest / len(pieces)))
        loudness = loudness * jnp.repeat(draws, extent[axis_at] // blocks).reshape([-1 if axis == axis_at else 1 for axis in range(len(extent))])
    return loudness


def profile(amount, total, bound, slope):
    portions = [(1 << 20) // math.isqrt(grade ** slope) + 1 for grade in range(2, amount + 1)]
    spare, counts = total - bound - (amount - 1), [1] * (amount - 1)
    while spare > 0:
        candidates = [i for i in range(amount - 1) if counts[i] < bound]
        whole, remaining = sum([portions[i] for i in candidates]), spare
        for i in candidates:
            more = min(bound - counts[i], max(1, remaining * portions[i] // whole), spare)
            counts[i] = counts[i] + more
            spare = spare - more
    return np.array([bound] + counts)


def uneven(stream_key, amount, total, most, slope):
    if amount == 2:
        one = jax.random.randint(stream_key, (), max(1, total - most), min(most, total - 1) + 1)
        return jnp.stack([one, total - one])
    sizes = jnp.asarray(profile(amount, total, most, slope), jnp.int32)
    pairs = (amount - 1) // 2
    giver, sink = sizes[1:1 + 2 * pairs:2], sizes[2:2 + 2 * pairs:2]
    room = jnp.minimum(giver - 1, most - sink)
    shifted = jax.random.randint(jax.random.fold_in(stream_key, 1), (pairs,), 0, 1 << 20) % (room + 1)
    sizes = sizes.at[1:1 + 2 * pairs:2].set(giver - shifted).at[2:2 + 2 * pairs:2].set(sink + shifted)
    return sizes[jax.random.permutation(jax.random.fold_in(stream_key, 2), amount)]


def noise(own_key, shape, deviation, reach, pieces=(), held_as=jnp.bfloat16):
    entries = jax.random.normal(own_key, shape, jnp.float32) * deviation
    if len(pieces) > 0:
        entries = block_levels(own_key, shape, pieces, -0.22, 0.18) * entries
    return jnp.clip(entries, min=-reach, max=reach).astype(held_as)


def setup_inputs(seed: int = 0) -> dict:
    streams_of = jax.random.split(jax.random.key(seed), 22)
    return {
        "tokens": noise(streams_of[0], (TOKENS, D), 1.0, 6.0, ((0, 32),)),
        "lengths": uneven(streams_of[1], SEQS, SEQS * SEQ * 5 // 8, SEQ, 0).astype(jnp.int32),
        "cotangent": noise(streams_of[2], (TOKENS, D), 1.0, 6.0, ((0, 32),)),
        "weight_qkv": noise(streams_of[3], (3 * D // GROUPS, D), (D // GROUPS) ** -0.5, 0.4375, ((1, 32),), jnp.float32),
        "weight_out": noise(streams_of[4], (D, D), (D // 32) ** -0.5, 1.25, ((1, 32),), jnp.float32),
        "weight_in": noise(streams_of[5], (D, FF // GROUPS), (D // GROUPS) ** -0.5, 0.4375, ((1, 32),), jnp.float32),
        "weight_down": noise(streams_of[6], (FF // GROUPS, D), (FF // GROUPS) ** -0.5, 0.21875, ((1, 32),), jnp.float32),
        "biases": noise(streams_of[7], (10, D), 0.2, 1.2, ((1, 32),), jnp.float32),
        "gains": jnp.clip(1.0 + 0.1 * jax.random.normal(streams_of[8], (2, D), jnp.float32), 0.5, 1.5),
        "first_qkv": noise(streams_of[9], (3 * D // GROUPS, D), ((TOKENS // 6) ** 0.5), 448.0, ((1, 32),), jnp.float32),
        "first_out": noise(streams_of[10], (D, D), ((TOKENS // 200) ** 0.5), 80.0, ((1, 32),), jnp.float32),
        "first_in": noise(streams_of[11], (D, FF // GROUPS), ((TOKENS // 30) ** 0.5), 192.0, ((1, 32),), jnp.float32),
        "first_down": noise(streams_of[12], (FF // GROUPS, D), ((TOKENS // 6) ** 0.5), 448.0, ((1, 32),), jnp.float32),
        "first_biases": noise(streams_of[13], (10, D), ((TOKENS // 9) ** 0.5), 384.0, ((1, 32),), jnp.float32),
        "first_gains": noise(streams_of[14], (2, D), ((TOKENS // 4) ** 0.5), 512.0, ((1, 32),), jnp.float32),
        "second_qkv": jnp.clip(jnp.exp(math.log(21845.0) - 1.3863401 * jax.random.uniform(streams_of[15], (3 * D // GROUPS, D), jnp.float32) ** block_levels(streams_of[15], (3 * D // GROUPS, D), ((1, 32),), -0.2, 0.2)), 5461.0, 21845.0),
        "second_out": jnp.clip(jnp.exp(math.log(655.0) - 1.390885 * jax.random.uniform(streams_of[16], (D, D), jnp.float32) ** block_levels(streams_of[16], (D, D), ((1, 32),), -0.2, 0.2)), 163.0, 655.0),
        "second_in": jnp.clip(jnp.exp(math.log(4369.0) - 1.3865233 * jax.random.uniform(streams_of[17], (D, FF // GROUPS), jnp.float32) ** block_levels(streams_of[17], (D, FF // GROUPS), ((1, 32),), -0.2, 0.2)), 1092.0, 4369.0),
        "second_down": jnp.clip(jnp.exp(math.log(21845.0) - 1.3863401 * jax.random.uniform(streams_of[18], (FF // GROUPS, D), jnp.float32) ** block_levels(streams_of[18], (FF // GROUPS, D), ((1, 32),), -0.2, 0.2)), 5461.0, 21845.0),
        "second_biases": jnp.clip(jnp.exp(math.log(14563.0) - 1.3865004 * jax.random.uniform(streams_of[19], (10, D), jnp.float32) ** block_levels(streams_of[19], (10, D), ((1, 32),), -0.2, 0.2)), 3640.0, 14563.0),
        "second_gains": jnp.clip(jnp.exp(math.log(32768.0) - 1.3862944 * jax.random.uniform(streams_of[20], (2, D), jnp.float32) ** block_levels(streams_of[20], (2, D), ((1, 32),), -0.2, 0.2)), 8192.0, 32768.0),
    }


@jax.custom_vjp
def low(v):
    return lax.optimization_barrier(v.astype(jnp.bfloat16)).astype(jnp.float32)

@jax.custom_vjp
def low_back(v):
    return v

def low_keep(v):
    return (low(v), None)

def low_pass(kept, grad):
    return (grad,)

def back_keep(v):
    return (v, None)

def back_low(kept, grad):
    return (low(grad),)
low.defvjp(low_keep, low_pass)
low_back.defvjp(back_keep, back_low)
highest = lax.Precision.HIGHEST
norm_eps = 1e-12
beta_rate = 0.5
adam_eps = 1e-08
step_rates = (0.1, 0.28, 0.1, 0.05, 0.3, 0.4)
decay_rates = (0.01, 0.01, 0.01, 0.01, 0.0, 0.0)
masked_score = -1000000000.0

def layer_norm(values, gain, shift):
    centred = values - lax.optimization_barrier(jnp.mean(values, axis=-1, keepdims=True))
    variance = lax.optimization_barrier(jnp.mean(centred * centred, axis=-1, keepdims=True))
    return centred * lax.rsqrt(variance + norm_eps) * gain + shift

def block_forward(rows, seq_lengths, params):
    weight_qkv, weight_out, weight_in, weight_down, biases, gains = params
    count = rows.shape[0]
    part = D // GROUPS
    wide = FF // GROUPS
    seq_count = count // SEQ
    grouped = rows.reshape(count, GROUPS, part)
    kernel = weight_qkv.reshape(3, part, GROUPS, part)
    projected = jnp.einsum('tgi,cogi->tcgo', grouped, kernel, precision=highest).reshape(count, 3, D)
    query = low(low_back(projected[:, 0] + biases[0]))
    keys = low(low_back(projected[:, 1]))
    values = low(low_back(projected[:, 2] + biases[1]))
    head_shape = (seq_count, SEQ, HEADS, HEAD)
    scores = jnp.einsum('bqhd,bkhd->bhqk', query.reshape(head_shape), keys.reshape(head_shape), precision=highest) * HEAD ** (-0.5)
    positions = jnp.arange(SEQ, dtype=jnp.int32)
    valid = positions[None, :] < seq_lengths[:, None]
    scores = low_back(jnp.where(valid[:, None, None, :], scores, masked_score))
    probs = low(jax.nn.softmax(scores, axis=-1))
    attended = jnp.einsum('bhqk,bkhd->bqhd', probs, values.reshape(head_shape), precision=highest).reshape(count, D)
    attended = low(low_back(attended))
    branch = low_back(jnp.dot(attended, weight_out, precision=highest) + biases[2])
    hidden = layer_norm(rows + branch, gains[0], biases[3 + GROUPS + 1])
    hidden_low = low(hidden)
    inner = jnp.einsum('tgi,gij->tgj', hidden_low.reshape(count, GROUPS, part), weight_in.reshape(GROUPS, part, wide), precision=highest).reshape(count, FF)
    inner = low_back(inner + biases[3:3 + GROUPS].reshape(FF))
    activated = low(jax.nn.gelu(inner, approximate=False))
    down = jnp.einsum('tgj,jgo->tgo', activated.reshape(count, GROUPS, wide), weight_down.reshape(wide, GROUPS, part), precision=highest).reshape(count, D)
    down = low_back(down + biases[3 + GROUPS])
    return layer_norm(hidden + down, gains[1], biases[3 + GROUPS + 2])

def adamw(weight, gradient, moment_one, moment_two, step_rate, decay_rate):
    new_one = beta_rate * moment_one + (1.0 - beta_rate) * gradient
    new_two = beta_rate * moment_two + (1.0 - beta_rate) * gradient * gradient
    correction = 1.0 - beta_rate ** STEP
    update = new_one / correction / (jnp.sqrt(new_two / correction) + adam_eps)
    return (new_one, new_two, weight - step_rate * (update + decay_rate * weight))

def reference(tokens, lengths, cotangent, weight_qkv, weight_out, weight_in, weight_down, biases, gains, first_qkv, first_out, first_in, first_down, first_biases, first_gains, second_qkv, second_out, second_in, second_down, second_biases, second_gains):
    masters = (weight_qkv, weight_out, weight_in, weight_down, biases, gains)
    firsts = (first_qkv, first_out, first_in, first_down, first_biases, first_gains)
    seconds = (second_qkv, second_out, second_in, second_down, second_biases, second_gains)
    block_count = SEQS // SEQ_DEV
    checked = jax.checkpoint(block_forward)

    def whole(rows, params):
        rounded = tuple((low(master) for master in params))

        def one_block(block_pair):
            return checked(block_pair[0], block_pair[1], rounded)
        results = lax.map(one_block, (rows.reshape(block_count, SEQ_DEV * SEQ, D), lengths.reshape(block_count, SEQ_DEV)))
        return results.reshape(TOKENS, D)
    output, pullback = jax.vjp(whole, tokens.astype(jnp.float32), masters)
    tokens_grad, gradients = pullback(cotangent.astype(jnp.float32))
    updated = [adamw(masters[number], gradients[number], firsts[number], seconds[number], step_rates[number], decay_rates[number]) for number in range(6)]
    return (output.astype(jnp.bfloat16), tokens_grad.astype(jnp.bfloat16), updated[0][0], updated[1][0], updated[2][0], updated[3][0], updated[4][0], updated[5][0], updated[0][1], updated[1][1], updated[2][1], updated[3][1], updated[4][1], updated[5][1], updated[0][2], updated[1][2], updated[2][2], updated[3][2], updated[4][2], updated[5][2])
```

```python
from functools import partial

import jax
import jax.numpy as jnp
from jax import lax
from jax.experimental import pallas as pl
from jax.experimental.pallas import tpu as pltpu
from jax.sharding import PartitionSpec as P

HEADS = 12
HEAD = 64
GROUPS = 4
SEQ = 512
STEP = 5


norm_eps = 1e-12
beta_rate = 0.5
adam_eps = 1e-08
step_rates = (0.1, 0.28, 0.1, 0.05, 0.3, 0.4)
decay_rates = (0.01, 0.01, 0.01, 0.01, 0.0, 0.0)
masked_score = -1000000000.0


MESH = pl.DeviceIdType.MESH
COLS = 24
WIDTHS = (640, 768, 768, 768)

def place():
    dp = lax.axis_index("dp"); fs = lax.axis_index("fsdp")
    return dp // 2, dp % 2, fs // 2, fs % 2

def device(y, x, z, c):
    return (y * 2 + x, z * 2 + c)

def greet(peers):
    barrier = pltpu.get_barrier_semaphore()
    for peer in peers:
        pl.semaphore_signal(barrier, inc=1, device_id=peer, device_id_type=MESH)
    pl.semaphore_wait(barrier, len(peers))

def all_peers():
    y, x, z, c = place()
    return [device(y, x, (z + d) % 4, c) for d in (1, 2, 3)] + [
        device(y, 1 - x, z, c), device(1 - y, x, z, c), device(y, x, z, 1 - c)]

def copy_to(src, dst, send, recv, peer):
    return pltpu.make_async_remote_copy(src_ref=src, dst_ref=dst, send_sem=send, recv_sem=recv, device_id=peer, device_id_type=MESH)

def gather_stage(stage, buf, send, recv):
    y, x, z, c = place()
    if stage == 0:
        mine = buf.at[y, x, z, c]
        return [copy_to(mine, mine, send.at[d - 1], recv.at[d - 1], device(y, x, (z + d) % 4, c)) for d in (1, 2, 3)]
    if stage == 1:
        one = buf.at[y, x, pl.ds(0, 2), c]
        two = buf.at[y, x, pl.ds(2, 2), c]
        return [copy_to(one, one, send.at[3], recv.at[3], device(y, 1 - x, z, c)),
                copy_to(two, two, send.at[4], recv.at[4], device(1 - y, x, z, c))]
    if stage == 2:
        one = buf.at[y, :, pl.ds(0, 2), c]
        two = buf.at[:, x, pl.ds(2, 2), c]
        return [copy_to(one, one, send.at[5], recv.at[5], device(1 - y, x, z, c)),
                copy_to(two, two, send.at[6], recv.at[6], device(y, 1 - x, z, c))]
    whole = buf.at[:, :, :, c]
    return [copy_to(whole, whole, send.at[7], recv.at[7], device(y, x, z, 1 - c))]

def gather_kernel(wq, wo, wi, wd, bs, gs, gq, go, gi, gd, send, recv):
    y, x, z, c = place()
    greet(all_peers())
    bufs = (gq, go, gi, gd)
    small = jnp.concatenate([wq[...].T, bs[...].T, gs[...].T, jnp.zeros((COLS, 640 - 588), jnp.float32)], axis=1)
    flights = [[None] * 4 for _ in range(4)]
    srcs = (None, wo, wi, wd)
    def begin(w, s):
        flights[w][s] = gather_stage(s, bufs[w], send.at[w], recv.at[w])
        for cp in flights[w][s]: cp.start()
    def end(w, s):
        for cp in flights[w][s]: cp.wait()
    for tick in range(8):
        for w in range(4):
            s = tick - w
            if s == 0:
                v = small if w == 0 else srcs[w][...].T
                bufs[w][y, x, z, c] = v.astype(jnp.bfloat16)
            if 0 <= s - 1 < 4: end(w, s - 1)
            if 0 <= s < 4: begin(w, s)

def gather_all(wq, wo, wi, wd, bs, gs):
    vm = pl.BlockSpec(memory_space=pltpu.VMEM)
    outs = pl.pallas_call(
        gather_kernel,
        out_shape=[jax.ShapeDtypeStruct((2, 2, 4, 2, COLS, L), jnp.bfloat16) for L in WIDTHS],
        in_specs=[vm] * 6, out_specs=[vm] * 4,
        scratch_shapes=[pltpu.SemaphoreType.DMA((4, 8)), pltpu.SemaphoreType.DMA((4, 8))],
        compiler_params=pltpu.CompilerParams(collective_id=0, has_side_effects=True, vmem_limit_bytes=48 << 20),
        name="gather_weights",
    )(wq, wo, wi, wd, bs, gs)
    return [o.reshape(768, -1) for o in outs]

def scatter_kernel(gq, go, gi, gd, oq, oo, oi, od, r1, r2a, r2b, r3, acc, send, recv):
    y, x, z, c = place()
    greet(all_peers())
    ins = (gq, go, gi, gd); outs = (oq, oo, oi, od)
    offs = [0, 640, 640 + 768, 640 + 2 * 768]
    flights = [[None] * 4 for _ in range(4)]
    def lanes(w): return pl.ds(offs[w], WIDTHS[w])
    f32 = jnp.float32
    def make(w, s):
        S, R, L = send.at[w], recv.at[w], lanes(w)
        if s == 0:
            return [copy_to(ins[w].at[:, :, :, 1 - c], r1.at[:, :, :, :, L], S.at[0], R.at[0], device(y, x, z, 1 - c))]
        if s == 1:
            return [copy_to(acc.at[:, 1 - x, pl.ds(0, 2), :, L], r2a.at[0, :, :, :, L], S.at[1], R.at[1], device(y, 1 - x, z, c)),
                    copy_to(acc.at[1 - y, :, pl.ds(2, 2), :, L], r2a.at[1, :, :, :, L], S.at[2], R.at[2], device(1 - y, x, z, c))]
        if s == 2:
            return [copy_to(acc.at[1 - y, x, pl.ds(0, 2), :, L], r2b.at[0, :, :, L], S.at[3], R.at[3], device(1 - y, x, z, c)),
                    copy_to(acc.at[y, 1 - x, pl.ds(2, 2), :, L], r2b.at[1, :, :, L], S.at[4], R.at[4], device(y, 1 - x, z, c))]
        return [copy_to(acc.at[y, x, (z + d) % 4, :, L], r3.at[d - 1, :, L], S.at[4 + d], R.at[4 + d], device(y, x, (z + d) % 4, c)) for d in (1, 2, 3)]
    def merge(w, s):
        L = lanes(w)
        if s == 0:
            def one(k, _):
                yy, xx, zz = k // 8, (k // 4) % 2, k % 4
                acc[yy, xx, zz, :, L] = (ins[w][yy, xx, zz, c].astype(f32) + r1[yy, xx, zz, :, L].astype(f32)).astype(jnp.bfloat16)
                return 0
            lax.fori_loop(0, 16, one, 0)
        if s == 1:
            for k in range(2):
                for zz in range(2):
                    acc[k, x, zz, :, L] = (acc[k, x, zz, :, L].astype(f32) + r2a[0, k, zz, :, L].astype(f32)).astype(jnp.bfloat16)
                    acc[y, k, 2 + zz, :, L] = (acc[y, k, 2 + zz, :, L].astype(f32) + r2a[1, k, zz, :, L].astype(f32)).astype(jnp.bfloat16)
        if s == 2:
            for zz in range(2):
                acc[y, x, zz, :, L] = (acc[y, x, zz, :, L].astype(f32) + r2b[0, zz, :, L].astype(f32)).astype(jnp.bfloat16)
                acc[y, x, 2 + zz, :, L] = (acc[y, x, 2 + zz, :, L].astype(f32) + r2b[1, zz, :, L].astype(f32)).astype(jnp.bfloat16)
        if s == 3:
            v = acc[y, x, z, :, L].astype(f32)
            for d in range(3): v = v + r3[d, :, L].astype(f32)
            outs[w][...] = v
    for tick in range(8):
        for w in range(4):
            s = tick - w
            if 0 <= s - 1 < 4:
                for cp in flights[w][s - 1]: cp.wait()
                merge(w, s - 1)
            if 0 <= s < 4:
                flights[w][s] = make(w, s)
                for cp in flights[w][s]: cp.start()

def scatter_all(grads):
    vm = pl.BlockSpec(memory_space=pltpu.VMEM)
    T = sum(WIDTHS); b = jnp.bfloat16
    return pl.pallas_call(
        scatter_kernel,
        out_shape=[jax.ShapeDtypeStruct((COLS, L), jnp.float32) for L in WIDTHS],
        in_specs=[vm] * 4, out_specs=[vm] * 4,
        scratch_shapes=[pltpu.VMEM((2, 2, 4, COLS, T), b), pltpu.VMEM((2, 2, 2, COLS, T), b), pltpu.VMEM((2, 2, COLS, T), b),
                        pltpu.VMEM((3, COLS, T), b), pltpu.VMEM((2, 2, 4, COLS, T), b),
                        pltpu.SemaphoreType.DMA((4, 8)), pltpu.SemaphoreType.DMA((4, 8))],
        compiler_params=pltpu.CompilerParams(collective_id=1, has_side_effects=True, vmem_limit_bytes=48 << 20),
        name="scatter_gradients",
    )(*[g.reshape(2, 2, 4, 2, COLS, g.shape[1]) for g in grads])


def fetch(masters):
    if lax.axis_size("dp") != 4 or lax.axis_size("fsdp") != 8:
        return tuple(
            lax.all_gather(master.astype(jnp.bfloat16), ("dp", "fsdp"), axis=1, tiled=True)
            for master in masters
        )
    first, out, inside, down = gather_all(*masters)
    return (
        first[:, :576].T,
        out.T,
        inside.T,
        down.T,
        first[:, 576:586].T,
        first[:, 586:588].T,
    )


def scatter_each(gradients):
    if lax.axis_size("dp") != 4 or lax.axis_size("fsdp") != 8:
        return tuple(
            lax.psum_scatter(gradient, ("dp", "fsdp"), scatter_dimension=1, tiled=True)
            for gradient in gradients
        )
    low = [gradient.astype(jnp.bfloat16).T for gradient in gradients]
    width = low[0].shape[0]
    first = jnp.concatenate(
        [low[0], low[4], low[5], jnp.zeros((width, 52), jnp.bfloat16)], axis=1
    )
    first, out, inside, down = scatter_all([first, low[1], low[2], low[3]])
    return (first[:, :576].T, out.T, inside.T, down.T, first[:, 576:586].T, first[:, 586:588].T)


def norm_forward(values, gain, shift):
    centred = values - jnp.mean(values, axis=1, keepdims=True)
    spread = lax.rsqrt(jnp.mean(centred * centred, axis=1, keepdims=True) + norm_eps)
    normed = centred * spread
    return (normed * gain + shift, normed, spread)


def norm_backward(upstream, normed, spread, gain):
    scaled = upstream * gain
    centred = (
        scaled
        - jnp.mean(scaled, axis=1, keepdims=True)
        - normed * jnp.mean(scaled * normed, axis=1, keepdims=True)
    )
    return (spread * centred, jnp.sum(upstream * normed, axis=0), jnp.sum(upstream, axis=0))


def seq_scores(query, keys, length):
    score_scale = HEAD ** (-0.5)
    scores = (
        jnp.einsum(
            "qhd,khd->hqk",
            query.reshape(SEQ, HEADS, HEAD),
            keys.reshape(SEQ, HEADS, HEAD),
            preferred_element_type=jnp.float32,
        )
        * score_scale
    )
    valid = jnp.arange(SEQ, dtype=jnp.int32) < length
    return jnp.where(valid[None, None, :], scores, masked_score)


def attend_forward(inputs_seq):
    query, keys, values, length = inputs_seq
    scores = seq_scores(query, keys, length)
    largest = jnp.max(scores, axis=-1, keepdims=True)
    log_sums = largest + jnp.log(jnp.sum(jnp.exp(scores - largest), axis=-1, keepdims=True))
    probs_low = jnp.exp(scores - log_sums).astype(jnp.bfloat16)
    attended = jnp.einsum(
        "hqk,khd->qhd",
        probs_low,
        values.reshape(SEQ, HEADS, HEAD),
        preferred_element_type=jnp.float32,
    )
    return (attended.reshape(SEQ, HEADS * HEAD).astype(jnp.bfloat16), log_sums)


def attend_backward(inputs_seq):
    query, keys, values, length, log_sums, upstream = inputs_seq
    score_scale = HEAD ** (-0.5)
    scores = seq_scores(query, keys, length)
    probs = jnp.exp(scores - log_sums)
    probs_low = probs.astype(jnp.bfloat16)
    heads_up = upstream.reshape(SEQ, HEADS, HEAD)
    prob_grad = jnp.einsum(
        "qhd,khd->hqk",
        heads_up,
        values.reshape(SEQ, HEADS, HEAD),
        preferred_element_type=jnp.float32,
    )
    value_grad = jnp.einsum("hqk,qhd->khd", probs_low, heads_up, preferred_element_type=jnp.float32)
    score_grad = (probs * (prob_grad - jnp.sum(prob_grad * probs, axis=-1, keepdims=True))).astype(
        jnp.bfloat16
    )
    query_grad = (
        jnp.einsum(
            "hqk,khd->qhd",
            score_grad,
            keys.reshape(SEQ, HEADS, HEAD),
            preferred_element_type=jnp.float32,
        )
        * score_scale
    )
    key_grad = (
        jnp.einsum(
            "hqk,qhd->khd",
            score_grad,
            query.reshape(SEQ, HEADS, HEAD),
            preferred_element_type=jnp.float32,
        )
        * score_scale
    )
    stacked = jnp.stack([query_grad, key_grad, value_grad], axis=1)
    return stacked.reshape(SEQ, 3, HEADS * HEAD).astype(jnp.bfloat16)


def layer_forward(rows, seq_lengths, weights):
    weight_qkv, weight_out, weight_in, weight_down, biases, gains = weights
    count, width = rows.shape
    part = width // GROUPS
    wide = weight_in.shape[1]
    seq_count = count // SEQ
    bias_f = biases.astype(jnp.float32)
    gain_f = gains.astype(jnp.float32)
    kernel = weight_qkv.reshape(3, part, GROUPS, part)
    projected = jnp.einsum(
        "tgi,cogi->tcgo",
        rows.reshape(count, GROUPS, part),
        kernel,
        preferred_element_type=jnp.float32,
    ).reshape(count, 3, width)
    query = (projected[:, 0] + bias_f[0]).astype(jnp.bfloat16)
    keys = projected[:, 1].astype(jnp.bfloat16)
    values = (projected[:, 2] + bias_f[1]).astype(jnp.bfloat16)
    shaped = (seq_count, SEQ, width)
    attended, log_sums = lax.map(
        attend_forward,
        (query.reshape(shaped), keys.reshape(shaped), values.reshape(shaped), seq_lengths),
    )
    attended = attended.reshape(count, width)
    branch = jnp.dot(attended, weight_out, preferred_element_type=jnp.float32) + bias_f[2]
    hidden, normed_one, spread_one = norm_forward(
        rows.astype(jnp.float32) + branch, gain_f[0], bias_f[3 + GROUPS + 1]
    )
    hidden_low = hidden.astype(jnp.bfloat16)
    inner = jnp.einsum(
        "tgi,gij->tgj",
        hidden_low.reshape(count, GROUPS, part),
        weight_in.reshape(GROUPS, part, wide),
        preferred_element_type=jnp.float32,
    ).reshape(count, GROUPS * wide)
    inner = inner + bias_f[3 : 3 + GROUPS].reshape(GROUPS * wide)
    activated = jax.nn.gelu(inner, approximate=False).astype(jnp.bfloat16)
    down = jnp.einsum(
        "tgj,jgo->tgo",
        activated.reshape(count, GROUPS, wide),
        weight_down.reshape(wide, GROUPS, part),
        preferred_element_type=jnp.float32,
    ).reshape(count, width)
    down = down + bias_f[3 + GROUPS]
    output, normed_two, spread_two = norm_forward(hidden + down, gain_f[1], bias_f[3 + GROUPS + 2])
    kept = (
        query,
        keys,
        values,
        log_sums,
        attended,
        normed_one,
        spread_one,
        hidden_low,
        inner,
        activated,
        normed_two,
        spread_two,
    )
    return (output, kept)


def layer_backward(rows, seq_lengths, upstream, weights, kept):
    weight_qkv, weight_out, weight_in, weight_down, biases, gains = weights
    (
        query,
        keys,
        values,
        log_sums,
        attended,
        normed_one,
        spread_one,
        hidden_low,
        inner,
        activated,
        normed_two,
        spread_two,
    ) = kept
    count, width = rows.shape
    part = width // GROUPS
    wide = weight_in.shape[1]
    seq_count = count // SEQ
    gain_f = gains.astype(jnp.float32)
    d_two, gain_two, shift_two = norm_backward(upstream, normed_two, spread_two, gain_f[1])
    down_grad = d_two.astype(jnp.bfloat16)
    grouped_down = down_grad.reshape(count, GROUPS, part)
    down_weight_grad = jnp.einsum(
        "tgj,tgo->jgo",
        activated.reshape(count, GROUPS, wide),
        grouped_down,
        preferred_element_type=jnp.float32,
    ).reshape(wide, width)
    act_grad = jnp.einsum(
        "tgo,jgo->tgj",
        grouped_down,
        weight_down.reshape(wide, GROUPS, part),
        preferred_element_type=jnp.float32,
    ).reshape(count, GROUPS * wide)
    unused_value, gelu_back = jax.vjp(partial(jax.nn.gelu, approximate=False), inner)
    inner_grad = gelu_back(act_grad)[0].astype(jnp.bfloat16)
    grouped_inner = inner_grad.reshape(count, GROUPS, wide)
    in_weight_grad = jnp.einsum(
        "tgi,tgj->gij",
        hidden_low.reshape(count, GROUPS, part),
        grouped_inner,
        preferred_element_type=jnp.float32,
    ).reshape(width, wide)
    hidden_grad = d_two + jnp.einsum(
        "tgj,gij->tgi",
        grouped_inner,
        weight_in.reshape(GROUPS, part, wide),
        preferred_element_type=jnp.float32,
    ).reshape(count, width)
    d_one, gain_one, shift_one = norm_backward(hidden_grad, normed_one, spread_one, gain_f[0])
    branch_grad = d_one.astype(jnp.bfloat16)
    out_weight_grad = jnp.einsum(
        "ti,to->io", attended, branch_grad, preferred_element_type=jnp.float32
    )
    attended_grad = jnp.einsum(
        "to,io->ti", branch_grad, weight_out, preferred_element_type=jnp.float32
    ).astype(jnp.bfloat16)
    shaped = (seq_count, SEQ, width)
    qkv_grad = lax.map(
        attend_backward,
        (
            query.reshape(shaped),
            keys.reshape(shaped),
            values.reshape(shaped),
            seq_lengths,
            log_sums,
            attended_grad.reshape(shaped),
        ),
    )
    grouped_qkv = qkv_grad.reshape(count, 3, GROUPS, part)
    qkv_weight_grad = jnp.einsum(
        "tgi,tcgo->cogi",
        rows.reshape(count, GROUPS, part),
        grouped_qkv,
        preferred_element_type=jnp.float32,
    ).reshape(3 * part, width)
    kernel = weight_qkv.reshape(3, part, GROUPS, part)
    rows_grad = d_one + jnp.einsum(
        "tcgo,cogi->tgi", grouped_qkv, kernel, preferred_element_type=jnp.float32
    ).reshape(count, width)
    qkv_sums = jnp.sum(qkv_grad.reshape(count, 3, width).astype(jnp.float32), axis=0)
    bias_grad = jnp.concatenate(
        [
            qkv_sums[0:1],
            qkv_sums[2:3],
            jnp.sum(branch_grad.astype(jnp.float32), axis=0)[None],
            jnp.sum(inner_grad.astype(jnp.float32), axis=0).reshape(GROUPS, wide),
            jnp.sum(down_grad.astype(jnp.float32), axis=0)[None],
            shift_one[None],
            shift_two[None],
        ],
        axis=0,
    )
    gain_grad = jnp.stack([gain_one, gain_two])
    return (
        rows_grad.astype(jnp.bfloat16),
        (qkv_weight_grad, out_weight_grad, in_weight_grad, down_weight_grad, bias_grad, gain_grad),
    )


def adamw(weight, gradient, moment_one, moment_two, step_rate, decay_rate):
    new_one = beta_rate * moment_one + (1.0 - beta_rate) * gradient
    new_two = beta_rate * moment_two + (1.0 - beta_rate) * gradient * gradient
    correction = 1.0 - beta_rate**STEP
    update = new_one / correction / (jnp.sqrt(new_two / correction) + adam_eps)
    return (new_one, new_two, weight - step_rate * (update + decay_rate * weight))


def body(
    tokens,
    lengths,
    cotangent,
    weight_qkv,
    weight_out,
    weight_in,
    weight_down,
    biases,
    gains,
    first_qkv,
    first_out,
    first_in,
    first_down,
    first_biases,
    first_gains,
    second_qkv,
    second_out,
    second_in,
    second_down,
    second_biases,
    second_gains,
):
    masters = (weight_qkv, weight_out, weight_in, weight_down, biases, gains)
    firsts = (first_qkv, first_out, first_in, first_down, first_biases, first_gains)
    seconds = (second_qkv, second_out, second_in, second_down, second_biases, second_gains)
    weights = fetch(masters)
    output, kept = layer_forward(tokens, lengths, weights)
    rows_grad, gradients = layer_backward(
        tokens, lengths, cotangent.astype(jnp.float32), weights, kept
    )
    total = scatter_each(gradients)
    updated = [
        adamw(
            masters[number],
            total[number],
            firsts[number],
            seconds[number],
            step_rates[number],
            decay_rates[number],
        )
        for number in range(6)
    ]
    return (
        output.astype(jnp.bfloat16),
        rows_grad,
        updated[0][0],
        updated[1][0],
        updated[2][0],
        updated[3][0],
        updated[4][0],
        updated[5][0],
        updated[0][1],
        updated[1][1],
        updated[2][1],
        updated[3][1],
        updated[4][1],
        updated[5][1],
        updated[0][2],
        updated[1][2],
        updated[2][2],
        updated[3][2],
        updated[4][2],
        updated[5][2],
    )


def solution(mesh):
    placed = (
        P(("dp", "fsdp"), None),
        P(("dp", "fsdp")),
        P(("dp", "fsdp"), None),
        P(None, ("dp", "fsdp")),
        P(None, ("dp", "fsdp")),
        P(None, ("dp", "fsdp")),
        P(None, ("dp", "fsdp")),
        P(None, ("dp", "fsdp")),
        P(None, ("dp", "fsdp")),
        P(None, ("dp", "fsdp")),
        P(None, ("dp", "fsdp")),
        P(None, ("dp", "fsdp")),
        P(None, ("dp", "fsdp")),
        P(None, ("dp", "fsdp")),
        P(None, ("dp", "fsdp")),
        P(None, ("dp", "fsdp")),
        P(None, ("dp", "fsdp")),
        P(None, ("dp", "fsdp")),
        P(None, ("dp", "fsdp")),
        P(None, ("dp", "fsdp")),
        P(None, ("dp", "fsdp")),
    )
    return jax.shard_map(
        body,
        mesh=mesh,
        in_specs=placed,
        out_specs=(
            P(("dp", "fsdp"), None),
            P(("dp", "fsdp"), None),
            P(None, ("dp", "fsdp")),
            P(None, ("dp", "fsdp")),
            P(None, ("dp", "fsdp")),
            P(None, ("dp", "fsdp")),
            P(None, ("dp", "fsdp")),
            P(None, ("dp", "fsdp")),
            P(None, ("dp", "fsdp")),
            P(None, ("dp", "fsdp")),
            P(None, ("dp", "fsdp")),
            P(None, ("dp", "fsdp")),
            P(None, ("dp", "fsdp")),
            P(None, ("dp", "fsdp")),
            P(None, ("dp", "fsdp")),
            P(None, ("dp", "fsdp")),
            P(None, ("dp", "fsdp")),
            P(None, ("dp", "fsdp")),
            P(None, ("dp", "fsdp")),
            P(None, ("dp", "fsdp")),
        ),
        check_vma=False,
    )
```

```python
import functools

import jax
import jax.numpy as jnp
from jax import lax
from jax.experimental import pallas as pl
from jax.experimental.pallas import tpu as pltpu
from jax.sharding import PartitionSpec as P

MESH = pl.DeviceIdType.MESH
COLS = 24
WIDTHS = (640, 768, 768, 768)

def place():
    dp = lax.axis_index("dp"); fs = lax.axis_index("fsdp")
    return dp // 2, dp % 2, fs // 2, fs % 2

def device(y, x, z, c):
    return (y * 2 + x, z * 2 + c)

def greet(peers):
    barrier = pltpu.get_barrier_semaphore()
    for peer in peers:
        pl.semaphore_signal(barrier, inc=1, device_id=peer, device_id_type=MESH)
    pl.semaphore_wait(barrier, len(peers))

def all_peers():
    y, x, z, c = place()
    return [device(y, x, (z + d) % 4, c) for d in (1, 2, 3)] + [
        device(y, 1 - x, z, c), device(1 - y, x, z, c), device(y, x, z, 1 - c)]

def copy_to(src, dst, send, recv, peer):
    return pltpu.make_async_remote_copy(src_ref=src, dst_ref=dst, send_sem=send, recv_sem=recv, device_id=peer, device_id_type=MESH)

def gather_stage(stage, buf, send, recv):
    y, x, z, c = place()
    if stage == 0:
        mine = buf.at[y, x, z, c]
        return [copy_to(mine, mine, send.at[d - 1], recv.at[d - 1], device(y, x, (z + d) % 4, c)) for d in (1, 2, 3)]
    if stage == 1:
        one = buf.at[y, x, pl.ds(0, 2), c]
        two = buf.at[y, x, pl.ds(2, 2), c]
        return [copy_to(one, one, send.at[3], recv.at[3], device(y, 1 - x, z, c)),
                copy_to(two, two, send.at[4], recv.at[4], device(1 - y, x, z, c))]
    if stage == 2:
        one = buf.at[y, :, pl.ds(0, 2), c]
        two = buf.at[:, x, pl.ds(2, 2), c]
        return [copy_to(one, one, send.at[5], recv.at[5], device(1 - y, x, z, c)),
                copy_to(two, two, send.at[6], recv.at[6], device(y, 1 - x, z, c))]
    whole = buf.at[:, :, :, c]
    return [copy_to(whole, whole, send.at[7], recv.at[7], device(y, x, z, 1 - c))]

def gather_kernel(wq, wo, wi, wd, bs, gs, gq, go, gi, gd, send, recv):
    y, x, z, c = place()
    greet(all_peers())
    bufs = (gq, go, gi, gd)
    small = jnp.concatenate([wq[...].T, bs[...].T, gs[...].T, jnp.zeros((COLS, 640 - 588), jnp.float32)], axis=1)
    flights = [[None] * 4 for _ in range(4)]
    srcs = (None, wo, wi, wd)
    def begin(w, s):
        flights[w][s] = gather_stage(s, bufs[w], send.at[w], recv.at[w])
        for cp in flights[w][s]: cp.start()
    def end(w, s):
        for cp in flights[w][s]: cp.wait()
    for tick in range(8):
        for w in range(4):
            s = tick - w
            if s == 0:
                v = small if w == 0 else srcs[w][...].T
                bufs[w][y, x, z, c] = v.astype(jnp.bfloat16)
            if 0 <= s - 1 < 4: end(w, s - 1)
            if 0 <= s < 4: begin(w, s)

def gather_all(wq, wo, wi, wd, bs, gs):
    vm = pl.BlockSpec(memory_space=pltpu.VMEM)
    outs = pl.pallas_call(
        gather_kernel,
        out_shape=[jax.ShapeDtypeStruct((2, 2, 4, 2, COLS, L), jnp.bfloat16) for L in WIDTHS],
        in_specs=[vm] * 6, out_specs=[vm] * 4,
        scratch_shapes=[pltpu.SemaphoreType.DMA((4, 8)), pltpu.SemaphoreType.DMA((4, 8))],
        compiler_params=pltpu.CompilerParams(collective_id=0, has_side_effects=True, vmem_limit_bytes=48 << 20),
        name="gather_weights",
    )(wq, wo, wi, wd, bs, gs)
    return [o.reshape(768, -1) for o in outs]

def scatter_kernel(gq, go, gi, gd, oq, oo, oi, od, r1, r2a, r2b, r3, acc, send, recv):
    y, x, z, c = place()
    greet(all_peers())
    ins = (gq, go, gi, gd); outs = (oq, oo, oi, od)
    offs = [0, 640, 640 + 768, 640 + 2 * 768]
    flights = [[None] * 4 for _ in range(4)]
    def lanes(w): return pl.ds(offs[w], WIDTHS[w])
    f32 = jnp.float32
    def make(w, s):
        S, R, L = send.at[w], recv.at[w], lanes(w)
        if s == 0:
            return [copy_to(ins[w].at[:, :, :, 1 - c], r1.at[:, :, :, :, L], S.at[0], R.at[0], device(y, x, z, 1 - c))]
        if s == 1:
            return [copy_to(acc.at[:, 1 - x, pl.ds(0, 2), :, L], r2a.at[0, :, :, :, L], S.at[1], R.at[1], device(y, 1 - x, z, c)),
                    copy_to(acc.at[1 - y, :, pl.ds(2, 2), :, L], r2a.at[1, :, :, :, L], S.at[2], R.at[2], device(1 - y, x, z, c))]
        if s == 2:
            return [copy_to(acc.at[1 - y, x, pl.ds(0, 2), :, L], r2b.at[0, :, :, L], S.at[3], R.at[3], device(1 - y, x, z, c)),
                    copy_to(acc.at[y, 1 - x, pl.ds(2, 2), :, L], r2b.at[1, :, :, L], S.at[4], R.at[4], device(y, 1 - x, z, c))]
        return [copy_to(acc.at[y, x, (z + d) % 4, :, L], r3.at[d - 1, :, L], S.at[4 + d], R.at[4 + d], device(y, x, (z + d) % 4, c)) for d in (1, 2, 3)]
    def merge(w, s):
        L = lanes(w)
        if s == 0:
            def one(k, _):
                yy, xx, zz = k // 8, (k // 4) % 2, k % 4
                acc[yy, xx, zz, :, L] = (ins[w][yy, xx, zz, c].astype(f32) + r1[yy, xx, zz, :, L].astype(f32)).astype(jnp.bfloat16)
                return 0
            lax.fori_loop(0, 16, one, 0)
        if s == 1:
            for k in range(2):
                for zz in range(2):
                    acc[k, x, zz, :, L] = (acc[k, x, zz, :, L].astype(f32) + r2a[0, k, zz, :, L].astype(f32)).astype(jnp.bfloat16)
                    acc[y, k, 2 + zz, :, L] = (acc[y, k, 2 + zz, :, L].astype(f32) + r2a[1, k, zz, :, L].astype(f32)).astype(jnp.bfloat16)
        if s == 2:
            for zz in range(2):
                acc[y, x, zz, :, L] = (acc[y, x, zz, :, L].astype(f32) + r2b[0, zz, :, L].astype(f32)).astype(jnp.bfloat16)
                acc[y, x, 2 + zz, :, L] = (acc[y, x, 2 + zz, :, L].astype(f32) + r2b[1, zz, :, L].astype(f32)).astype(jnp.bfloat16)
        if s == 3:
            v = acc[y, x, z, :, L].astype(f32)
            for d in range(3): v = v + r3[d, :, L].astype(f32)
            outs[w][...] = v
    for tick in range(8):
        for w in range(4):
            s = tick - w
            if 0 <= s - 1 < 4:
                for cp in flights[w][s - 1]: cp.wait()
                merge(w, s - 1)
            if 0 <= s < 4:
                flights[w][s] = make(w, s)
                for cp in flights[w][s]: cp.start()

def scatter_all(grads):
    vm = pl.BlockSpec(memory_space=pltpu.VMEM)
    T = sum(WIDTHS); b = jnp.bfloat16
    return pl.pallas_call(
        scatter_kernel,
        out_shape=[jax.ShapeDtypeStruct((COLS, L), jnp.float32) for L in WIDTHS],
        in_specs=[vm] * 4, out_specs=[vm] * 4,
        scratch_shapes=[pltpu.VMEM((2, 2, 4, COLS, T), b), pltpu.VMEM((2, 2, 2, COLS, T), b), pltpu.VMEM((2, 2, COLS, T), b),
                        pltpu.VMEM((3, COLS, T), b), pltpu.VMEM((2, 2, 4, COLS, T), b),
                        pltpu.SemaphoreType.DMA((4, 8)), pltpu.SemaphoreType.DMA((4, 8))],
        compiler_params=pltpu.CompilerParams(collective_id=1, has_side_effects=True, vmem_limit_bytes=48 << 20),
        name="scatter_gradients",
    )(*[g.astype(jnp.bfloat16).reshape(2, 2, 4, 2, COLS, g.shape[1]) for g in grads])

f32, bf16 = jnp.float32, jnp.bfloat16
SEQ = 512; HEADS = 12; HEAD = 64; PART = 192; NG = 4; D = 768
NT = (((1,), (1,)), ((), ()))
NN = (((1,), (0,)), ((), ()))
def dot(a, b, dims=NN):
    return lax.dot_general(a, b, dims, preferred_element_type=f32)
def aligned(v, m): return pl.multiple_of(v, m)

def transpose_in(x, xt):
    for s in range(2):
        xt[:, s * SEQ:(s + 1) * SEQ] = x[s * SEQ:(s + 1) * SEQ, :].T

def project(gq, xt, qkv, wqt):
    def one(g, _):
        rows = pl.ds(aligned(g * PART, PART), PART)
        wqt[...] = gq[rows, :].T
        bias_q = gq[rows, 576:577].astype(f32)
        bias_v = gq[rows, 577:578].astype(f32)
        for s in range(2):
            lanes = slice(s * SEQ, (s + 1) * SEQ)
            xg = xt[rows, lanes]
            qkv[g, 0:192, lanes] = ((dot(wqt[0:192], xg) + bias_q).astype(bf16) * 0.125).astype(bf16)
            qkv[g, 192:384, lanes] = dot(wqt[192:384], xg).astype(bf16)
            qkv[g, 384:576, lanes] = (dot(wqt[384:576], xg) + bias_v).astype(bf16)
        return 0
    lax.fori_loop(0, NG, one, 0)

def head_place(n):
    s = n // HEADS; h = n % HEADS
    g = h // 3; r = (h % 3) * HEAD
    return s, g, r

def heads_forward(m, nh, lengths, qkv, probs, att):
    st = []
    for j in range(nh):
        n = m * nh + j
        s, g, r = head_place(n)
        lanes = pl.ds(aligned(s * SEQ, SEQ), SEQ)
        q = qkv[g, pl.ds(aligned(r, HEAD), HEAD), lanes]
        k = qkv[g, pl.ds(aligned(192 + r, HEAD), HEAD), lanes]
        v = qkv[g, pl.ds(aligned(384 + r, HEAD), HEAD), lanes]
        st.append((n, s, g, r, lanes, q, k, v))
    scs = [dot(k.T, q) for (n, s, g, r, lanes, q, k, v) in st]
    ps = []
    for (n, s, g, r, lanes, q, k, v), sc in zip(st, scs):
        valid = lax.broadcasted_iota(jnp.int32, (SEQ, 1), 0) < lengths[s]
        sc = jnp.where(valid, sc, -1e9)
        m_ = jnp.max(sc, axis=0, keepdims=True)
        e = jnp.exp(sc - m_)
        inv = 1.0 / jnp.sum(e, axis=0, keepdims=True)
        p = (e * inv).astype(bf16)
        probs[n] = p
        ps.append(p)
    for (n, s, g, r, lanes, q, k, v), p in zip(st, ps):
        att[pl.ds(aligned(g * PART + r, HEAD), HEAD), lanes] = dot(v, p)

FNH = 2
def front_kernel(lengths, x, gq, xt, qkv, probs, att, wqt):
    transpose_in(x, xt)
    project(gq, xt, qkv, wqt)
    def one(n, _):
        heads_forward(n, FNH, lengths, qkv, probs, att)
        return 0
    lax.fori_loop(0, 2 * HEADS // FNH, one, 0)

VM = pl.BlockSpec(memory_space=pltpu.VMEM)
SM = pl.BlockSpec(memory_space=pltpu.SMEM)
def front(lengths, x, gq):
    S = jax.ShapeDtypeStruct
    return pl.pallas_call(front_kernel,
        out_shape=[S((768, 1024), bf16), S((4, 576, 1024), bf16), S((24, 512, 512), bf16), S((768, 1024), f32)],
        in_specs=[SM, VM, VM], out_specs=[VM] * 4,
        scratch_shapes=[pltpu.VMEM((640, 192), bf16)],
        compiler_params=pltpu.CompilerParams(vmem_limit_bytes=56 << 20), name="front")(lengths, x, gq)


CH = 16
def each(total, body, init=None, step=CH, unroll=2):
    def one(i, carry):
        return body(pl.ds(aligned(i * step, step), step), carry)
    return lax.fori_loop(0, total // step, one, init, unroll=unroll)

def fold_rows(v):
    return v.reshape(v.shape[0] // 8, 8, v.shape[1]).sum(axis=0)

def total_rows(v):
    return jnp.sum(v, axis=0, keepdims=True)

def lane_sum(v):
    acc = v[:, 0:128]
    for i in range(1, v.shape[1] // 128):
        acc = acc + v[:, i * 128:(i + 1) * 128]
    return jnp.sum(acc, axis=1, keepdims=True)

RSQRT2 = 0.7071067811865476
INV_SQRT_2PI = 0.3989422804014327

def gelu_both(x):
    cdf = 0.5 * (1.0 + lax.erf(x * RSQRT2))
    pdf = jnp.exp(-0.5 * x * x) * INV_SQRT_2PI
    return x * cdf, cdf + x * pdf

def prep_weights(go, gi, gd, wot, wit, wi4, wd4):
    wot[...] = go[...].T
    wit[...] = gi[...].T
    for g in range(NG):
        wi4[g] = gi[:, g * PART:(g + 1) * PART]
        wd4[g] = gd[g * PART:(g + 1) * PART, :].T

def column(gq, rows, v):
    return gq[rows, 576 + v:577 + v].astype(f32)

T = 1024
def stats(total, square):
    mean = total * (1.0 / D)
    return mean

def mid_forward(gq, go, gd, xt, attb, wi4, H, D2, hlow, ACT, GP, rs):
    H[...] = dot(go[...], attb[...])
    def a(rows, acc):
        r = xt[rows, :].astype(f32) + (H[rows, :] + column(gq, rows, 2))
        H[rows, :] = r
        return acc + fold_rows(r)
    mean = total_rows(each(D, a, jnp.zeros((8, T), f32))) * (1.0 / D)
    def b(rows, acc):
        c = H[rows, :] - mean
        return acc + fold_rows(c * c)
    rstd = lax.rsqrt(total_rows(each(D, b, jnp.zeros((8, T), f32))) * (1.0 / D) + 1e-12)
    rs[0:1, :] = rstd
    def c(rows, acc):
        n = (H[rows, :] - mean) * rstd
        H[rows, :] = n
        hlow[rows, :] = (n * column(gq, rows, 10) + column(gq, rows, 8)).astype(bf16)
        return acc
    each(D, c, 0)
    def group(g, acc):
        grows = pl.ds(aligned(g * PART, PART), PART)
        h = hlow[grows, :]
        for j in range(3):
            jr = pl.ds(j * 256, 256)
            D2[0:256, :] = dot(wi4[g, jr, :], h)
            def e(rows, acc):
                out = pl.ds(aligned(j * 256 + rows.start, CH), CH)
                bias = gq[out, 576:640].astype(f32)
                lane = lax.broadcasted_iota(jnp.int32, (1, 64), 1)
                bias = jnp.sum(jnp.where(lane == 3 + g, bias, 0.0), axis=1, keepdims=True)
                act, gp = gelu_both(D2[rows, :] + bias)
                ACT[g, out, :] = act.astype(bf16)
                GP[g, out, :] = gp.astype(bf16)
                return acc
            each(256, e, 0)
        return acc
    lax.fori_loop(0, NG, group, 0)
    def group2(g, acc):
        grows = pl.ds(aligned(g * PART, PART), PART)
        D2[grows, :] = dot(gd[grows, :], ACT[g])
        return acc
    lax.fori_loop(0, NG, group2, 0)

def mid_turn(gq, cott, H, D2, outt, DD, dgq, rs):
    z = jnp.zeros((8, T), f32)
    def a(rows, acc):
        r = (H[rows, :] * column(gq, rows, 10) + column(gq, rows, 8)) + (D2[rows, :] + column(gq, rows, 7))
        D2[rows, :] = r
        return acc + fold_rows(r)
    mean = total_rows(each(D, a, z)) * (1.0 / D)
    def b(rows, acc):
        c = D2[rows, :] - mean
        return acc + fold_rows(c * c)
    rstd = lax.rsqrt(total_rows(each(D, b, z)) * (1.0 / D) + 1e-12)
    def c(rows, acc):
        n = (D2[rows, :] - mean) * rstd
        D2[rows, :] = n
        gain = column(gq, rows, 11)
        outt[rows, :] = (n * gain + column(gq, rows, 9)).astype(bf16)
        u = cott[rows, :].astype(f32)
        e = u * gain
        un = u * n
        dgq[rows, 587:588] = lane_sum(un)
        dgq[rows, 585:586] = lane_sum(u)
        return (acc[0] + fold_rows(e), acc[1] + fold_rows(e * n))
    se, sen = each(D, c, (z, z))
    me, men = total_rows(se) * (1.0 / D), total_rows(sen) * (1.0 / D)
    def d(rows, acc):
        e = cott[rows, :].astype(f32) * column(gq, rows, 11)
        g = rstd * (e - me - D2[rows, :] * men)
        D2[rows, :] = g
        low = g.astype(bf16)
        DD[rows, :] = low
        dgq[rows, 583:584] = lane_sum(low.astype(f32))
        return acc
    each(D, d, 0)

def mid_backward(gq, wd4, wit, hlow, ACT, GP, DD, D2, IG, dgd, dgi, dgq):
    for g in range(NG):
        grows = slice(g * PART, (g + 1) * PART)
        for j in range(3):
            jr = slice(j * 256, (j + 1) * 256)
            ag = dot(wd4[g, jr, :], DD[grows, :])
            low = (ag * GP[g, jr, :].astype(f32)).astype(bf16)
            IG[jr, :] = low
            dgq[jr, 579 + g:580 + g] = lane_sum(low.astype(f32))
        dgd[grows, :] = lax.dot_general(DD[grows, :], ACT[g], NT, preferred_element_type=f32).astype(bf16)
        dgi[:, grows] = lax.dot_general(IG[...], hlow[grows, :], NT, preferred_element_type=f32).astype(bf16)
        D2[grows, :] = D2[grows, :] + dot(wit[grows, :], IG[...])

def mid_close(gq, wot, attb, H, D2, DB, dat, dgo, dgq, rs):
    z = jnp.zeros((8, T), f32)
    def a(rows, acc):
        u, n = D2[rows, :], H[rows, :]
        e = u * column(gq, rows, 10)
        dgq[rows, 586:587] = lane_sum(u * n)
        dgq[rows, 584:585] = lane_sum(u)
        return (acc[0] + fold_rows(e), acc[1] + fold_rows(e * n))
    se, sen = each(D, a, (z, z))
    me, men = total_rows(se) * (1.0 / D), total_rows(sen) * (1.0 / D)
    rstd = rs[0:1, :]
    def d(rows, acc):
        e = D2[rows, :] * column(gq, rows, 10)
        g = rstd * (e - me - H[rows, :] * men)
        D2[rows, :] = g
        low = g.astype(bf16)
        DB[rows, :] = low
        dgq[rows, 578:579] = lane_sum(low.astype(f32))
        return acc
    each(D, d, 0)
    dat[...] = dot(wot[...], DB[...]).astype(bf16)
    dgo[...] = lax.dot_general(DB[...], attb[...], NT, preferred_element_type=f32).astype(bf16)

def mid_kernel(xt, att, cot, gq, go, gi, gd, out, dat, done, dgq, dgo, dgi, dgd,
               attb, cott, H, D2, hlow, ACT, GP, DD, IG, wot, wit, wi4, wd4, rs):
    prep_weights(go, gi, gd, wot, wit, wi4, wd4)
    attb[...] = att[...].astype(bf16)
    transpose_in(cot, cott)
    mid_forward(gq, go, gd, xt, attb, wi4, H, D2, hlow, ACT, GP, rs)
    outt = attb_alias = IG
    mid_turn(gq, cott, H, D2, outt, DD, dgq, rs)
    for s in range(2):
        out[s * SEQ:(s + 1) * SEQ, :] = outt[:, s * SEQ:(s + 1) * SEQ].T
    mid_backward(gq, wd4, wit, hlow, ACT, GP, DD, D2, IG, dgd, dgi, dgq)
    mid_close(gq, wot, attb, H, D2, DD, dat, dgo, dgq, rs)
    done[...] = D2[...].astype(done.dtype)

def mid_scratch():
    V = pltpu.VMEM
    A = lambda: V((D, T), bf16)
    F = lambda: V((D, T), f32)
    return [A(), A(), F(), F(), A(), V((4, D, T), bf16), V((4, D, T), bf16), A(), A(),
            V((D, D), bf16), V((D, D), bf16), V((4, D, PART), bf16), V((4, D, PART), bf16), V((8, T), f32)]

def mid(xt, att, cot, gq, go, gi, gd):
    S = jax.ShapeDtypeStruct
    return pl.pallas_call(mid_kernel,
        out_shape=[S((T, D), bf16), S((D, T), bf16), S((D, T), f32), S((D, 640), f32), S((D, D), bf16), S((D, D), bf16), S((D, D), bf16)],
        in_specs=[VM] * 7, out_specs=[VM] * 7, scratch_shapes=mid_scratch(),
        compiler_params=pltpu.CompilerParams(vmem_limit_bytes=62 << 20), name="mid")(xt, att, cot, gq, go, gi, gd)

def heads_backward(m, nh, qkv, probs, att, dat, dqkv):
    st = []
    for j in range(nh):
        n = m * nh + j
        s, g, r = head_place(n)
        lanes = pl.ds(aligned(s * SEQ, SEQ), SEQ)
        hr = pl.ds(aligned(g * PART + r, HEAD), HEAD)
        q = qkv[g, pl.ds(aligned(r, HEAD), HEAD), lanes]
        k = qkv[g, pl.ds(aligned(192 + r, HEAD), HEAD), lanes]
        v = qkv[g, pl.ds(aligned(384 + r, HEAD), HEAD), lanes]
        up = dat[hr, lanes]
        inner = jnp.sum(up.astype(f32) * att[hr, lanes], axis=0, keepdims=True)
        st.append((n, g, r, lanes, q, k, v, up, inner))
    dps = [dot(v.T, up) for (n, g, r, lanes, q, k, v, up, inner) in st]
    dss = []
    for (n, g, r, lanes, q, k, v, up, inner), dp in zip(st, dps):
        dss.append((probs[n].astype(f32) * (dp - inner)).astype(bf16))
    for (n, g, r, lanes, q, k, v, up, inner), ds in zip(st, dss):
        dqkv[g, pl.ds(aligned(384 + r, HEAD), HEAD), lanes] = lax.dot_general(up, probs[n], NT, preferred_element_type=f32).astype(bf16)
        dqkv[g, pl.ds(aligned(r, HEAD), HEAD), lanes] = (dot(k, ds) * 0.125).astype(bf16)
        dqkv[g, pl.ds(aligned(192 + r, HEAD), HEAD), lanes] = lax.dot_general(q, ds, NT, preferred_element_type=f32).astype(bf16)

def finish_group(g, gq, xt, dqkv, done, dgq, tg):
    grows = pl.ds(aligned(g * PART, PART), PART)
    dq = dqkv[g]
    dgq[grows, 0:576] = lax.dot_general(xt[grows, :], dq, NT, preferred_element_type=f32)
    dgq[grows, 576:577] = lane_sum(dqkv[g, 0:192, :].astype(f32))
    dgq[grows, 577:578] = lane_sum(dqkv[g, 384:576, :].astype(f32))
    tg[grows, :] = (done[grows, :] + dot(gq[grows, 0:576], dq)).astype(bf16)

BNH = 2
def back_kernel(qkv, probs, att, dat, xt, done, gq, dgq_in, tgrad, dgq, dqkv, tg):
    dgq[...] = dgq_in[...]
    def one(m, _):
        heads_backward(m, BNH, qkv, probs, att, dat, dqkv)
        return 0
    lax.fori_loop(0, 24 // BNH, one, 0)
    def fin(g, _):
        finish_group(g, gq, xt, dqkv, done, dgq, tg)
        return 0
    lax.fori_loop(0, NG, fin, 0)
    for s in range(2):
        tgrad[s * SEQ:(s + 1) * SEQ, :] = tg[:, s * SEQ:(s + 1) * SEQ].T

def back(qkv, probs, att, dat, xt, done, gq, dgq):
    S = jax.ShapeDtypeStruct
    return pl.pallas_call(back_kernel,
        out_shape=[S((T, D), bf16), S((D, 640), f32)],
        in_specs=[VM] * 8, out_specs=[VM] * 2,
        scratch_shapes=[pltpu.VMEM((4, 576, T), bf16), pltpu.VMEM((D, T), bf16)],
        compiler_params=pltpu.CompilerParams(vmem_limit_bytes=62 << 20), name="back")(qkv, probs, att, dat, xt, done, gq, dgq)


step_rates = (0.1, 0.28, 0.1, 0.05, 0.3, 0.4)
decay_rates = (0.01, 0.01, 0.01, 0.01, 0.0, 0.0)


def adam_kernel(*refs):
    grads, refs = refs[:4], refs[4:]
    weights, firsts, seconds, outs = refs[:6], refs[6:12], refs[12:18], refs[18:]
    low = grads[0][...].T
    parts = (low[0:576], None, None, None, low[576:586], low[586:588])
    correction = 1.0 - 0.5**5
    for i in range(6):
        grad = grads[i][...].T if parts[i] is None else parts[i]
        weight = weights[i][...]
        one = 0.5 * firsts[i][...] + 0.5 * grad
        two = 0.5 * seconds[i][...] + 0.5 * grad * grad
        update = one / correction / (jnp.sqrt(two / correction) + 1e-08)
        outs[i][...] = one
        outs[6 + i][...] = two
        outs[12 + i][...] = weight - step_rates[i] * (update + decay_rates[i] * weight)


def adam(sums, masters, firsts, seconds):
    shapes = [jax.ShapeDtypeStruct(m.shape, f32) for m in masters]
    return pl.pallas_call(
        adam_kernel,
        out_shape=shapes * 3,
        in_specs=[VM] * 22,
        out_specs=[VM] * 18,
        compiler_params=pltpu.CompilerParams(vmem_limit_bytes=40 << 20),
        name="adam",
    )(*sums, *masters, *firsts, *seconds)


def own_links():
    return lax.axis_size("dp") == 4 and lax.axis_size("fsdp") == 8


def fetch(masters):
    if own_links():
        return gather_all(*masters)
    full = [lax.all_gather(m.astype(bf16), ("dp", "fsdp"), axis=1, tiled=True).T for m in masters]
    first = jnp.concatenate([full[0], full[4], full[5], jnp.zeros((D, 52), bf16)], axis=1)
    return first, full[1], full[2], full[3]


def combine(grads):
    if own_links():
        return scatter_all(grads)
    return [
        lax.psum_scatter(g.astype(f32), ("dp", "fsdp"), scatter_dimension=0, tiled=True)
        for g in grads
    ]


def body(tokens, lengths, cotangent, *state):
    masters, firsts, seconds = state[:6], state[6:12], state[12:]
    gq, go, gi, gd = fetch(masters)
    xt, qkv, probs, att = front(lengths, tokens, gq)
    output, dat, done, dgq, dgo, dgi, dgd = mid(xt, att, cotangent, gq, go, gi, gd)
    tokens_grad, dgq = back(qkv, probs, att, dat, xt, done, gq, dgq)
    sums = combine((dgq, dgo, dgi, dgd))
    return (output, tokens_grad, *adam(sums, masters, firsts, seconds))


def solution(mesh):
    rows, columns = P(("dp", "fsdp"), None), P(None, ("dp", "fsdp"))
    return jax.shard_map(
        body,
        mesh=mesh,
        in_specs=(rows, P(("dp", "fsdp")), rows) + (columns,) * 18,
        out_specs=(rows, rows) + (columns,) * 18,
        check_vma=False,
    )
```
